32 devices in a mesh: groups: 2 (over y), store: 8 (over z, x), tensor: 2 (over core).
Axes of the slice: x: 2, y: 2, z: 4, core: 2. Of those that a mesh axis runs over, the one named last changes fastest.
Arguments:
- queries: bfloat16 [32, 8192], P(('groups', 'store'), 'tensor'), parts along dimension 0, may hold values from -200 to 200
- new_kv: bfloat16 [32, 2, 1024], P(('groups', 'store'), None, 'tensor'), parts along dimension 0, may hold values from -15 to 15
- kv_pages: bfloat16 [128, 2, 256, 1024], P(('groups', 'store'), None, None, 'tensor'), parts along dimension 0, may hold values from -15 to 15
- page_index: int32 [32, 4], P(('groups', 'store')), parts along dimension 0, may hold values from 0 to 7
- page_owner: int32 [32, 4], P(('groups', 'store')), parts along dimension 0, may hold values from 0 to 7, as said below
- seq_pages: int32 [32], P(('groups', 'store')), parts along dimension 0, may hold values from 1 to 4, as said below
Outputs:
- attended: bfloat16 [32, 8192], P(('groups', 'store'), 'tensor'), parts along dimension 0
The draws below stay inside these ranges and needn't reach their ends.
There are 2 independent parts, one for each index of `groups`. The reference program is written for one: setup_inputs(seed, part) draws one part's arguments, and reference() takes and returns one part's arrays. A program takes and returns all parts, laid end to end along the dimension named above; each array names one. Nothing has to cross between parts.
Inputs may be any that keep to these rules, and one draw needn't show every extreme that they name: `page_owner`: page j of sequence s lies on store index (s // 2 + o) modulo the number of store indices, with o from 0 to 3; over the slots of the sequences of one store index, at most 2 share one o, so at most 2 live pages of those sequences lie on one store index. `seq_pages`: the sequences of store index 0 all have 4 pages.
All inputs are finite; a program needn't handle non-finite values.
Results may differ from the reference program's by a relative error of at most 0.0011.
Values may be sent and summed in bfloat16 or wider, within the bound.
No kernel may reach another device: no remote copies, remote signals or barrier semaphores. Data moves between devices by JAX's collectives and lax.ppermute only.
A program may use at most 64 MiB of HBM per device.

```python
import jax
import jax.numpy as jnp
from jax import lax

HEADS = 64
KV_HEADS = 8
HEAD_DIM = 128
PAGE = 256
MAXP = 4
B_DEV = 2
GROUP = 8
CAP = 2
P_DEV = 8
SEQS = 16
PAGES = 64


def draw_queries(key, part):
    first = jax.random.fold_in(key, 0)
    base = jax.random.normal(first, (SEQS, HEADS * HEAD_DIM), jnp.float32)
    return jnp.clip(base, -200.0, 200.0).astype(jnp.bfloat16)


def draw_page_owner(key, part):
    shards = SEQS // B_DEV
    entries = B_DEV * MAXP
    keys = jax.random.split(jax.random.fold_in(key, 11), shards)
    orders = jax.vmap(lambda single: jax.random.permutation(single, entries))(keys)
    page_starts = orders // CAP
    shard_holders = (jnp.arange(shards, dtype=jnp.int32)[:, None] + page_starts) % shards
    return shard_holders.reshape(SEQS, MAXP).astype(jnp.int32)


def draw_seq_pages(key, part):
    counts = jax.random.randint(jax.random.fold_in(key, 23), (SEQS,), 1, MAXP + 1, dtype=jnp.int32)
    return counts.at[:B_DEV].set(MAXP)


def plant(drawn, key, low, high):
    index_at = [jax.random.randint(jax.random.fold_in(key, axis), (), 0, length) for axis, length in enumerate(drawn.shape)]
    widest = drawn.shape.index(max(drawn.shape))
    next_to = index_at[:widest] + [(index_at[widest] + 1) % drawn.shape[widest]] + index_at[widest + 1:]
    return drawn.at[tuple(index_at)].set(low).at[tuple(next_to)].set(high)


def level_of(key, dims, cuts, smallest, top_value):
    def one(axis_at, blocks):
        steps = jax.random.uniform(jax.random.fold_in(jax.random.fold_in(key, 6), axis_at), (blocks,), jnp.float32, smallest / len(cuts), top_value / len(cuts))
        return jnp.repeat(jnp.exp(steps), dims[axis_at] // blocks).reshape((-1,) + (1,) * (len(dims) - axis_at - 1))

    level = one(*cuts[0])
    for cut in cuts[1:]:
        level = level * one(*cut)
    return level


def centred(key, shape, scale, reach, cuts=(), kind=jnp.bfloat16):
    array = jax.random.normal(key, shape, jnp.float32) * scale
    if len(cuts) > 0:
        array = level_of(key, shape, cuts, -0.22, 0.18) * array
    return jnp.clip(array, min=-reach, max=reach).astype(kind)


def setup_inputs(seed: int = 0, part: int = 0) -> dict:
    splits = jax.random.split(jax.random.key(seed), 7)
    part_splits = jax.random.split(jax.random.fold_in(splits[6], part), 7)
    queries = draw_queries(jax.random.fold_in(jax.random.fold_in(splits[6], part), 71), part)
    new_kv = centred(part_splits[1], (SEQS, 2, KV_HEADS * HEAD_DIM), 2.5, 15.0, ((0, 8), (2, 2)))
    kv_pages = centred(part_splits[2], (PAGES, 2, PAGE, KV_HEADS * HEAD_DIM), 2.5, 15.0, ((0, 8), (3, 2)))
    page_index = plant(jax.random.randint(part_splits[3], (SEQS, MAXP), 0, P_DEV), jax.random.fold_in(part_splits[3], 1), 0, P_DEV - 1).astype(jnp.int32)
    page_owner = draw_page_owner(jax.random.fold_in(jax.random.fold_in(splits[6], part), 71), part)
    seq_pages = draw_seq_pages(jax.random.fold_in(jax.random.fold_in(splits[6], part), 71), part)
    return {"queries": queries, "new_kv": new_kv, "kv_pages": kv_pages, "page_index": page_index, "page_owner": page_owner, "seq_pages": seq_pages}


def reference(queries, new_kv, kv_pages, page_index, page_owner, seq_pages):
    scale = HEAD_DIM ** -0.5

    def single_request_attend(items):
        query, fresh, places, shard_holders, length = items
        rows = (shard_holders * P_DEV + places).astype(jnp.int32)
        chosen = kv_pages[rows]
        keys = chosen[:, 0].reshape(MAXP * PAGE, KV_HEADS, HEAD_DIM).astype(jnp.float32)
        values = chosen[:, 1].reshape(MAXP * PAGE, KV_HEADS, HEAD_DIM).astype(jnp.float32)
        live = (jnp.arange(MAXP * PAGE, dtype=jnp.int32) // PAGE) < length
        heads = query.reshape(KV_HEADS, GROUP, HEAD_DIM).astype(jnp.float32)
        new_key = fresh[0].reshape(KV_HEADS, HEAD_DIM).astype(jnp.float32)
        new_value = fresh[1].reshape(KV_HEADS, HEAD_DIM).astype(jnp.float32)
        scores = jnp.einsum("kgd,pkd->kgp", heads, keys, precision=lax.Precision.HIGHEST) * scale
        own = jnp.einsum("kgd,kd->kg", heads, new_key, precision=lax.Precision.HIGHEST) * scale
        masked = jnp.where(live[None, None, :], scores, jnp.float32(-1e30))
        peak = jnp.maximum(jnp.max(masked, axis=-1), own)
        weights = jnp.where(live[None, None, :], jnp.exp(masked - peak[..., None]), jnp.float32(0.0))
        own_weight = jnp.exp(own - peak)
        total = jnp.sum(weights, axis=-1) + own_weight
        summed = jnp.einsum("kgp,pkd->kgd", weights, values, precision=lax.Precision.HIGHEST)
        summed = summed + own_weight[..., None] * new_value[:, None, :]
        return (summed / total[..., None]).reshape(-1).astype(jnp.bfloat16)

    return lax.map(single_request_attend, (queries, new_kv, page_index, page_owner, seq_pages))
```

```python
import functools

import jax
import jax.numpy as jnp
from jax import lax
from jax.experimental import pallas as pl
from jax.experimental.pallas import tpu as pltpu
from jax.sharding import PartitionSpec as P

HEAD_DIM = 128
REACH = 4
TILE = 8
PACKED_TILE = 16
NEVER = -1e30
VMEM = pl.BlockSpec(memory_space=pltpu.VMEM)
PARAMS = pltpu.CompilerParams(vmem_limit_bytes=16 * 2**20)
SMEM = pl.BlockSpec(memory_space=pltpu.SMEM)


def shifted(value, axis, steps):
    count = lax.axis_size(axis)
    pairs = [(source, (source + steps) % count) for source in range(count)]
    return lax.ppermute(value, axis, pairs)


def slot_plan(owner_ref, length_ref, places_ref, count, capacity):
    myself = lax.axis_index("store")
    seq_count, most_pages = owner_ref.shape
    zero = jnp.int32(0)
    plan = [[(zero, zero, zero) for _ in range(capacity)] for _ in range(REACH)]
    taken = [zero for _ in range(REACH)]
    for seq in range(seq_count):
        for page in range(most_pages):
            live = page < length_ref[seq]
            gap = owner_ref[seq, page] - myself
            gap = jnp.where(gap < 0, gap + count, gap)
            place = places_ref[seq, page] if places_ref is not None else zero
            for step in range(REACH):
                mine = live & (gap == step)
                for slot in range(capacity):
                    here = mine & (taken[step] == slot)
                    old = plan[step][slot]
                    plan[step][slot] = (
                        jnp.where(here, jnp.int32(seq), old[0]),
                        jnp.where(here, place, old[1]),
                        jnp.where(here, jnp.int32(1), old[2]),
                    )
                taken[step] = taken[step] + mine.astype(jnp.int32)
    return plan


def first_kernel(out_ref):
    out_ref[...] = jnp.zeros_like(out_ref)


def pack_kernel(count, capacity, first_ref, owner_ref, length_ref, places_ref, queries_ref, *refs):
    outs, rows = refs[:-1], refs[-1]
    seq_count = queries_ref.shape[0]
    heads = queries_ref.shape[1] // HEAD_DIM
    for head in range(heads):
        rows[pl.ds(head, seq_count, stride=heads), :] = queries_ref[
            :, head * HEAD_DIM : (head + 1) * HEAD_DIM
        ].astype(jnp.float32)
    plan = slot_plan(owner_ref, length_ref, places_ref, count, capacity)
    line = lax.broadcasted_iota(jnp.int32, (PACKED_TILE, HEAD_DIM), 0)
    for step in range(REACH):
        note = jnp.zeros((PACKED_TILE, HEAD_DIM), jnp.int32)
        for slot in range(capacity):
            seq, place, _ = plan[step][slot]
            value = rows[0:heads, :]
            for other in range(1, seq_count):
                value = jnp.where(seq == other, rows[other * heads : (other + 1) * heads, :], value)
            outs[step][slot * heads : (slot + 1) * heads, :] = value.astype(jnp.bfloat16)
            note = jnp.where(line == slot, place, note)
        outs[step][capacity * heads :, :] = note.astype(jnp.float32).astype(jnp.bfloat16)


def page_parts(payload_ref, pages_ref, slot, heads, capacity, scale):
    kv_count = pages_ref.shape[3] // HEAD_DIM
    group = heads // kv_count
    notes = payload_ref[capacity * heads :, :].astype(jnp.float32)
    place = notes[slot, 0].astype(jnp.int32)
    query = payload_ref[slot * heads : (slot + 1) * heads, :].astype(jnp.float32)
    row_group = lax.broadcasted_iota(jnp.int32, query.shape, 0) // group
    spread = jnp.concatenate(
        [jnp.where(row_group == kv, query, 0.0) for kv in range(kv_count)], axis=1
    ).astype(jnp.bfloat16)
    scores = lax.dot_general(
        spread, pages_ref[place, 0], (((1,), (1,)), ((), ())), preferred_element_type=jnp.float32
    ) * scale
    peak = jnp.max(scores, axis=1, keepdims=True)
    weights = jnp.exp(scores - peak)
    total = jnp.sum(weights, axis=1, keepdims=True)
    high = weights.astype(jnp.bfloat16)
    low = (weights - high.astype(jnp.float32)).astype(jnp.bfloat16)
    both = jnp.dot(
        jnp.concatenate([high, low], axis=0), pages_ref[place, 1], preferred_element_type=jnp.float32
    )
    wide = both[:heads] + both[heads:]
    summed = [
        wide[kv * group : (kv + 1) * group, kv * HEAD_DIM : (kv + 1) * HEAD_DIM]
        for kv in range(kv_count)
    ]
    return peak, total, jnp.concatenate(summed, axis=0)


def to_lanes(column, offset):
    shape = (column.shape[0], HEAD_DIM)
    at = lax.broadcasted_iota(jnp.int32, shape, 0) + offset
    lane = lax.broadcasted_iota(jnp.int32, shape, 1)
    return jnp.sum(jnp.where(at == lane, column, 0.0), axis=0, keepdims=True)


def to_column(row, offset, heads):
    shape = (heads, HEAD_DIM)
    at = lax.broadcasted_iota(jnp.int32, shape, 0) + offset
    lane = lax.broadcasted_iota(jnp.int32, shape, 1)
    return jnp.sum(jnp.where(at == lane, row, 0.0), axis=1, keepdims=True)


def attend_kernel(heads, capacity, scale, payload_ref, pages_ref, out_ref):
    row = jnp.zeros((1, HEAD_DIM), jnp.float32)
    for slot in range(capacity):
        peak, total, summed = page_parts(payload_ref, pages_ref, slot, heads, capacity, scale)
        out_ref[slot * heads : (slot + 1) * heads, :] = summed
        row = row + to_lanes(peak, slot * heads) + to_lanes(total, (capacity + slot) * heads)
    out_ref[capacity * heads :, :] = jnp.broadcast_to(row, (TILE, HEAD_DIM))


def local_kernel(
    count, capacity, scale, owner_ref, length_ref, queries_ref, fresh_ref, payload_ref, pages_ref,
    state_ref, bias_ref, rows
):
    seq_count = queries_ref.shape[0]
    heads = queries_ref.shape[1] // HEAD_DIM
    kv_count = fresh_ref.shape[2] // HEAD_DIM
    group = heads // kv_count
    plan = slot_plan(owner_ref, length_ref, None, count, capacity)
    for head in range(heads):
        rows[pl.ds(head, seq_count, stride=heads), :] = queries_ref[
            :, head * HEAD_DIM : (head + 1) * HEAD_DIM
        ].astype(jnp.float32)
    slots = [
        (plan[0][slot][0], plan[0][slot][2])
        + page_parts(payload_ref, pages_ref, slot, heads, capacity, scale)
        for slot in range(capacity)
    ]
    row = jnp.zeros((1, HEAD_DIM), jnp.float32)
    for seq in range(seq_count):
        query = rows[seq * heads : (seq + 1) * heads, :]

        def fresh(which):
            line = fresh_ref[seq, which : which + 1, :].astype(jnp.float32)
            return jnp.concatenate(
                [
                    jnp.broadcast_to(line[:, kv * HEAD_DIM : (kv + 1) * HEAD_DIM], (group, HEAD_DIM))
                    for kv in range(kv_count)
                ],
                axis=0,
            )

        own = jnp.sum(query * fresh(0), axis=1, keepdims=True) * scale
        highest = own
        for at, used, peak, _, _ in slots:
            inside = (used > 0) & (at == seq)
            highest = jnp.maximum(highest, jnp.where(inside, peak, NEVER))
        own_weight = jnp.exp(own - highest)
        denominator = own_weight
        numerator = own_weight * fresh(1)
        for at, used, peak, total, summed in slots:
            inside = (used > 0) & (at == seq)
            factor = jnp.exp(jnp.where(inside, peak - highest, NEVER))
            denominator = denominator + factor * total
            numerator = numerator + factor * summed
        state_ref[seq * heads : (seq + 1) * heads, :] = numerator
        row = row + to_lanes(highest, seq * heads) + to_lanes(denominator, (seq_count + seq) * heads)
    state_ref[seq_count * heads :, :] = jnp.broadcast_to(row, (TILE, HEAD_DIM))
    line = lax.broadcasted_iota(jnp.int32, (TILE, HEAD_DIM), 0)
    lane = lax.broadcasted_iota(jnp.int32, (TILE, HEAD_DIM), 1)
    for step in range(1, REACH):
        bias = jnp.full((TILE, HEAD_DIM), NEVER, jnp.float32)
        for slot in range(capacity):
            at, _, used = plan[step][slot]
            mine = (line == at) & (lane // heads == slot) & (used > 0)
            bias = jnp.where(mine, 0.0, bias)
        bias_ref[(step - 1) * TILE : step * TILE, :] = bias


def combine_kernel(seq_count, capacity, state_ref, bias_ref, *refs):
    parts, out_ref, rows = refs[:-2], refs[-2], refs[-1]
    heads = out_ref.shape[1] // HEAD_DIM
    state_row = state_ref[seq_count * heads : seq_count * heads + 1, :]
    for seq in range(seq_count):
        base = to_column(state_row, seq * heads, heads)
        highest = base
        slots = []
        for step, part in enumerate(parts):
            row = part[capacity * heads : capacity * heads + 1, :]
            masked = row + bias_ref[step * TILE + seq : step * TILE + seq + 1, :]
            for slot in range(capacity):
                peak = to_column(masked, slot * heads, heads)
                total = to_column(row, (capacity + slot) * heads, heads)
                slots.append((peak, total, part[slot * heads : (slot + 1) * heads, :]))
                highest = jnp.maximum(highest, peak)
        factor = jnp.exp(base - highest)
        denominator = factor * to_column(state_row, (seq_count + seq) * heads, heads)
        numerator = factor * state_ref[seq * heads : (seq + 1) * heads, :]
        for peak, total, summed in slots:
            factor = jnp.exp(peak - highest)
            denominator = denominator + factor * total
            numerator = numerator + factor * summed
        rows[seq * heads : (seq + 1) * heads, :] = numerator / denominator
    for head in range(heads):
        out_ref[:, head * HEAD_DIM : (head + 1) * HEAD_DIM] = rows[
            pl.ds(head, seq_count, stride=heads), :
        ].astype(jnp.bfloat16)


def body(queries, new_kv, kv_pages, page_index, page_owner, seq_pages):
    count = lax.axis_size("store")
    seq_count, most_pages = page_index.shape
    capacity = seq_count * most_pages // REACH
    heads = queries.shape[1] // HEAD_DIM
    scale = HEAD_DIM ** (-0.5)
    slot_rows = capacity * heads
    assert kv_pages.shape[0] <= 256 and 2 * slot_rows <= HEAD_DIM and seq_count <= TILE
    sent = jax.ShapeDtypeStruct((slot_rows + PACKED_TILE, HEAD_DIM), jnp.bfloat16)
    back = jax.ShapeDtypeStruct((slot_rows + TILE, HEAD_DIM), jnp.float32)
    scratch = [pltpu.VMEM((seq_count * heads, HEAD_DIM), jnp.float32)]
    first = pl.pallas_call(
        first_kernel,
        out_shape=jax.ShapeDtypeStruct((TILE, HEAD_DIM), jnp.float32),
        out_specs=VMEM,
        compiler_params=PARAMS,
        cost_estimate=pl.CostEstimate(flops=2*10**9, bytes_accessed=0, transcendentals=0),
        name="first",
    )()
    payloads = pl.pallas_call(
        functools.partial(pack_kernel, count, capacity),
        out_shape=[sent] * REACH,
        in_specs=[VMEM] + [SMEM] * 3 + [VMEM],
        out_specs=[VMEM] * REACH,
        scratch_shapes=scratch,
        compiler_params=PARAMS,
        name="pack",
        cost_estimate=pl.CostEstimate(flops=10**12, bytes_accessed=0, transcendentals=0),
    )(first, page_owner, seq_pages, page_index, queries)
    attend = pl.pallas_call(
        functools.partial(attend_kernel, heads, capacity, scale),
        out_shape=back,
        in_specs=[VMEM] * 2,
        out_specs=VMEM,
        compiler_params=PARAMS,
        name="attend",
    )
    pages = kv_pages
    parts = [
        shifted(attend(shifted(payloads[step], "store", step), pages), "store", -step)
        for step in range(1, REACH)
    ]
    state, bias = pl.pallas_call(
        functools.partial(local_kernel, count, capacity, scale),
        out_shape=[
            jax.ShapeDtypeStruct((seq_count * heads + TILE, HEAD_DIM), jnp.float32),
            jax.ShapeDtypeStruct(((REACH - 1) * TILE, HEAD_DIM), jnp.float32),
        ],
        in_specs=[SMEM] * 2 + [VMEM] * 4,
        out_specs=[VMEM] * 2,
        scratch_shapes=scratch,
        compiler_params=PARAMS,
        name="local",
    )(page_owner, seq_pages, queries, new_kv, payloads[0], pages)
    return pl.pallas_call(
        functools.partial(combine_kernel, seq_count, capacity),
        out_shape=jax.ShapeDtypeStruct(queries.shape, queries.dtype),
        in_specs=[VMEM] * (1 + REACH),
        out_specs=VMEM,
        scratch_shapes=scratch,
        compiler_params=PARAMS,
        name="combine",
    )(state, bias, *parts)


def solution(mesh):
    in_specs = (
        P(("groups", "store"), "tensor"),
        P(("groups", "store"), None, "tensor"),
        P(("groups", "store"), None, None, "tensor"),
        P(("groups", "store"), None),
        P(("groups", "store"), None),
        P(("groups", "store")),
    )
    out_specs = P(("groups", "store"), "tensor")
    return jax.shard_map(body, mesh=mesh, in_specs=in_specs, out_specs=out_specs, check_vma=False)
```

```python
import functools

import jax
import jax.numpy as jnp
from jax import lax
from jax.experimental import pallas as pl
from jax.experimental.pallas import tpu as pltpu
from jax.sharding import PartitionSpec as P

HEAD_DIM = 128
REACH = 4
TILE = 8
PACKED_TILE = 16
NEVER = -1e30
FIELD = 256
VMEM = pl.BlockSpec(memory_space=pltpu.VMEM)
SMEM = pl.BlockSpec(memory_space=pltpu.SMEM)
PARAMS = pltpu.CompilerParams(vmem_limit_bytes=16 * 2**20)


def shifted(value, axis, steps):
    count = lax.axis_size(axis)
    pairs = [(source, (source + steps) % count) for source in range(count)]
    return lax.ppermute(value, axis, pairs)


def slot_plan(owner_ref, length_ref, places_ref, count, capacity):
    myself = lax.axis_index("store")
    seq_count, most_pages = owner_ref.shape
    codes = [[jnp.int32(0)] * capacity for _ in range(REACH)]
    for seq in reversed(range(seq_count)):
        for page in reversed(range(most_pages)):
            gap = owner_ref[seq, page] - myself
            gap = jnp.where(gap < 0, gap + count, gap)
            gap = jnp.where(page < length_ref[seq], gap, jnp.int32(-1))
            code = jnp.int32((FIELD + seq) * FIELD)
            if places_ref is not None:
                code = code + places_ref[seq, page]
            for step in range(REACH):
                mine = gap == step
                slots = codes[step]
                codes[step] = [
                    jnp.where(mine, code if slot == 0 else slots[slot - 1], slots[slot])
                    for slot in range(capacity)
                ]
    return [
        [((code // FIELD) % FIELD, code % FIELD, code // (FIELD * FIELD)) for code in slots]
        for slots in codes
    ]


def spread_rows(queries_ref, rows):
    seq_count = queries_ref.shape[0]
    heads = queries_ref.shape[1] // HEAD_DIM
    for head in range(heads):
        rows[pl.ds(head, seq_count, stride=heads), :] = queries_ref[
            :, head * HEAD_DIM : (head + 1) * HEAD_DIM
        ].astype(jnp.float32)


def slot_rows(rows, seq, heads):
    return rows[pl.ds(pl.multiple_of(seq * heads, TILE), heads), :]


def first_kernel(out_ref):
    out_ref[...] = jnp.zeros_like(out_ref)


def pack_kernel(count, capacity, first_ref, owner_ref, length_ref, places_ref, queries_ref, *refs):
    outs, rows = refs[:-1], refs[-1]
    heads = queries_ref.shape[1] // HEAD_DIM
    spread_rows(queries_ref, rows)
    plan = slot_plan(owner_ref, length_ref, places_ref, count, capacity)
    line = lax.broadcasted_iota(jnp.int32, (PACKED_TILE, HEAD_DIM), 0)
    for step in range(1, REACH):
        out_ref = outs[step - 1]
        note = jnp.zeros((PACKED_TILE, HEAD_DIM), jnp.int32)
        for slot in range(capacity):
            seq, place, _ = plan[step][slot]
            out_ref[slot * heads : (slot + 1) * heads, :] = slot_rows(rows, seq, heads).astype(jnp.bfloat16)
            note = jnp.where(line == slot, place, note)
        out_ref[capacity * heads :, :] = note.astype(jnp.float32).astype(jnp.bfloat16)


def page_parts(slots, pages_ref, scale):
    kv_count = pages_ref.shape[3] // HEAD_DIM
    group = slots[0][0].shape[0] // kv_count
    scores = [
        jnp.concatenate(
            [
                lax.dot_general(
                    query[kv * group : (kv + 1) * group, :],
                    pages_ref[place, 0, :, kv * HEAD_DIM : (kv + 1) * HEAD_DIM],
                    (((1,), (1,)), ((), ())),
                    preferred_element_type=jnp.float32,
                )
                for kv in range(kv_count)
            ],
            axis=0,
        )
        * scale
        for query, place in slots
    ]
    peaks = [jnp.max(score, axis=1, keepdims=True) for score in scores]
    weights = [jnp.exp(score - peak) for score, peak in zip(scores, peaks)]
    totals = [jnp.sum(weight, axis=1, keepdims=True) for weight in weights]
    sums = []
    for weight, (_, place) in zip(weights, slots):
        high = weight.astype(jnp.bfloat16).astype(jnp.float32)
        low = weight - high
        parts = []
        for kv in range(kv_count):
            mine = slice(kv * group, (kv + 1) * group)
            both = jnp.dot(
                jnp.concatenate([high[mine], low[mine]], axis=0).astype(jnp.bfloat16),
                pages_ref[place, 1, :, kv * HEAD_DIM : (kv + 1) * HEAD_DIM],
                preferred_element_type=jnp.float32,
            )
            parts.append(both[:group] + both[group:])
        sums.append(jnp.concatenate(parts, axis=0))
    return list(zip(peaks, totals, sums))


def to_lanes(column, offset):
    shape = (column.shape[0], HEAD_DIM)
    at = lax.broadcasted_iota(jnp.int32, shape, 0) + offset
    lane = lax.broadcasted_iota(jnp.int32, shape, 1)
    return jnp.where(at == lane, column, 0.0)


def to_column(row, offset, heads):
    shape = (heads, HEAD_DIM)
    at = lax.broadcasted_iota(jnp.int32, shape, 0) + offset
    lane = lax.broadcasted_iota(jnp.int32, shape, 1)
    return jnp.sum(jnp.where(at == lane, row, 0.0), axis=1, keepdims=True)


def attend_kernel(heads, capacity, scale, payload_ref, pages_ref, out_ref):
    notes = payload_ref[capacity * heads :, :].astype(jnp.float32)
    slots = [
        (payload_ref[slot * heads : (slot + 1) * heads, :], notes[slot, 0].astype(jnp.int32))
        for slot in range(capacity)
    ]
    marks = jnp.zeros((heads, HEAD_DIM), jnp.float32)
    for slot, (peak, total, summed) in enumerate(page_parts(slots, pages_ref, scale)):
        out_ref[slot * heads : (slot + 1) * heads, :] = summed
        marks = marks + to_lanes(peak, slot * heads) + to_lanes(total, (capacity + slot) * heads)
    row = jnp.sum(marks, axis=0, keepdims=True)
    out_ref[capacity * heads :, :] = jnp.broadcast_to(row, (TILE, HEAD_DIM))


def local_kernel(
    count, capacity, scale, owner_ref, length_ref, places_ref, queries_ref, fresh_ref, pages_ref,
    state_ref, bias_ref, rows
):
    seq_count = queries_ref.shape[0]
    heads = queries_ref.shape[1] // HEAD_DIM
    kv_count = fresh_ref.shape[2] // HEAD_DIM
    group = heads // kv_count
    spread_rows(queries_ref, rows)
    plan = slot_plan(owner_ref, length_ref, places_ref, count, capacity)
    local = page_parts(
        [(slot_rows(rows, seq, heads).astype(jnp.bfloat16), place) for seq, place, _ in plan[0]],
        pages_ref,
        scale,
    )
    line = lax.broadcasted_iota(jnp.int32, (TILE, HEAD_DIM), 0)
    lane = lax.broadcasted_iota(jnp.int32, (TILE, HEAD_DIM), 1)
    peaks = jnp.full((TILE, HEAD_DIM), NEVER, jnp.float32)
    totals = jnp.zeros((TILE, HEAD_DIM), jnp.float32)
    for seq in range(seq_count):
        query = rows[seq * heads : (seq + 1) * heads, :]

        def fresh(which):
            new = fresh_ref[seq, which : which + 1, :].astype(jnp.float32)
            return jnp.concatenate(
                [
                    jnp.broadcast_to(new[:, kv * HEAD_DIM : (kv + 1) * HEAD_DIM], (group, HEAD_DIM))
                    for kv in range(kv_count)
                ],
                axis=0,
            )

        own = jnp.sum(query * fresh(0), axis=1, keepdims=True) * scale
        highest = own
        for (at, _, used), (peak, _, _) in zip(plan[0], local):
            highest = jnp.maximum(highest, jnp.where((used > 0) & (at == seq), peak, NEVER))
        own_weight = jnp.exp(own - highest)
        denominator = own_weight
        numerator = own_weight * fresh(1)
        for (at, _, used), (peak, total, summed) in zip(plan[0], local):
            inside = (used > 0) & (at == seq)
            factor = jnp.exp(jnp.where(inside, peak - highest, NEVER))
            denominator = denominator + factor * total
            numerator = numerator + factor * summed
        state_ref[seq * heads : (seq + 1) * heads, :] = numerator
        high_row = jnp.sum(to_lanes(highest, 0), axis=0, keepdims=True)
        total_row = jnp.sum(to_lanes(denominator, 0), axis=0, keepdims=True)
        peaks = jnp.where((line == seq) & (lane < heads), high_row, peaks)
        totals = jnp.where(line == seq, total_row, totals)
    bias_ref[0:TILE, :] = peaks
    for step in range(1, REACH):
        bias = jnp.full((TILE, HEAD_DIM), NEVER, jnp.float32)
        for slot in range(capacity):
            at, _, used = plan[step][slot]
            mine = (line == at) & (lane // heads == slot) & (used > 0)
            bias = jnp.where(mine, 0.0, bias)
        bias_ref[step * TILE : (step + 1) * TILE, :] = bias
    bias_ref[REACH * TILE :, :] = totals


def combine_kernel(seq_count, capacity, state_ref, bias_ref, *refs):
    parts, out_ref, rows = refs[:-2], refs[-2], refs[-1]
    heads = out_ref.shape[1] // HEAD_DIM
    marks = [part[capacity * heads :, :] for part in parts]
    peaks = [bias_ref[0:TILE, :]] + [
        mark + bias_ref[(at + 1) * TILE : (at + 2) * TILE, :] for at, mark in enumerate(marks)
    ]
    totals = [bias_ref[REACH * TILE :, :]] + [
        pltpu.roll(mark, HEAD_DIM - capacity * heads, 1) for mark in marks
    ]

    def over_slots(tile, join):
        whole = tile
        for slot in range(1, capacity):
            whole = join(whole, pltpu.roll(tile, slot * heads, 1))
            whole = join(whole, pltpu.roll(tile, HEAD_DIM - slot * heads, 1))
        return whole

    highest = over_slots(functools.reduce(jnp.maximum, peaks), jnp.maximum)
    factors = [jnp.exp(peak - highest) for peak in peaks]
    share = functools.reduce(jnp.add, [factor * total for factor, total in zip(factors, totals)])
    inverse = 1.0 / over_slots(share, jnp.add)
    factors = [factor * inverse for factor in factors]
    for seq in range(seq_count):
        line = slice(seq, seq + 1)
        numerator = to_column(factors[0][line], 0, heads) * state_ref[seq * heads : (seq + 1) * heads, :]
        for factor, part in zip(factors[1:], parts):
            for slot in range(capacity):
                column = to_column(factor[line], slot * heads, heads)
                numerator = numerator + column * part[slot * heads : (slot + 1) * heads, :]
        rows[seq * heads : (seq + 1) * heads, :] = numerator
    for head in range(heads):
        out_ref[:, head * HEAD_DIM : (head + 1) * HEAD_DIM] = rows[
            pl.ds(head, seq_count, stride=heads), :
        ].astype(jnp.bfloat16)


def body(queries, new_kv, kv_pages, page_index, page_owner, seq_pages):
    count = lax.axis_size("store")
    seq_count, most_pages = page_index.shape
    capacity = seq_count * most_pages // REACH
    heads = queries.shape[1] // HEAD_DIM
    scale = HEAD_DIM ** (-0.5)
    rows = capacity * heads
    assert kv_pages.shape[0] <= FIELD and seq_count <= TILE
    assert 2 * rows <= HEAD_DIM and heads % TILE == 0
    sent = jax.ShapeDtypeStruct((rows + PACKED_TILE, HEAD_DIM), jnp.bfloat16)
    back = jax.ShapeDtypeStruct((rows + TILE, HEAD_DIM), jnp.float32)
    scratch = [pltpu.VMEM((seq_count * heads, HEAD_DIM), jnp.float32)]
    first = pl.pallas_call(
        first_kernel,
        out_shape=jax.ShapeDtypeStruct((TILE, HEAD_DIM), jnp.float32),
        out_specs=VMEM,
        compiler_params=PARAMS,
        cost_estimate=pl.CostEstimate(flops=2 * 10**9, bytes_accessed=0, transcendentals=0),
        name="first",
    )()
    payloads = pl.pallas_call(
        functools.partial(pack_kernel, count, capacity),
        out_shape=[sent] * (REACH - 1),
        in_specs=[VMEM] + [SMEM] * 3 + [VMEM],
        out_specs=[VMEM] * (REACH - 1),
        scratch_shapes=scratch,
        compiler_params=PARAMS,
        cost_estimate=pl.CostEstimate(flops=10**12, bytes_accessed=0, transcendentals=0),
        name="pack",
    )(first, page_owner, seq_pages, page_index, queries)
    attend = pl.pallas_call(
        functools.partial(attend_kernel, heads, capacity, scale),
        out_shape=back,
        in_specs=[VMEM] * 2,
        out_specs=VMEM,
        compiler_params=PARAMS,
        name="attend",
    )
    parts = []
    for step in range(1, REACH):
        payload = shifted(payloads[step - 1], "store", step)
        part = attend(payload, kv_pages)
        parts.append(shifted(part, "store", -step))
    state, bias = pl.pallas_call(
        functools.partial(local_kernel, count, capacity, scale),
        out_shape=[
            jax.ShapeDtypeStruct((seq_count * heads, HEAD_DIM), jnp.float32),
            jax.ShapeDtypeStruct(((REACH + 1) * TILE, HEAD_DIM), jnp.float32),
        ],
        in_specs=[SMEM] * 3 + [VMEM] * 3,
        out_specs=[VMEM] * 2,
        scratch_shapes=scratch,
        compiler_params=PARAMS,
        name="local",
    )(page_owner, seq_pages, page_index, queries, new_kv, kv_pages)
    return pl.pallas_call(
        functools.partial(combine_kernel, seq_count, capacity),
        out_shape=jax.ShapeDtypeStruct(queries.shape, queries.dtype),
        in_specs=[VMEM] * (1 + REACH),
        out_specs=VMEM,
        scratch_shapes=scratch,
        compiler_params=PARAMS,
        name="combine",
    )(state, bias, *parts)


def solution(mesh):
    in_specs = (
        P(("groups", "store"), "tensor"),
        P(("groups", "store"), None, "tensor"),
        P(("groups", "store"), None, None, "tensor"),
        P(("groups", "store"), None),
        P(("groups", "store"), None),
        P(("groups", "store")),
    )
    out_specs = P(("groups", "store"), "tensor")

    return jax.shard_map(body, mesh=mesh, in_specs=in_specs, out_specs=out_specs, check_vma=False)
```

```python
import functools

import jax
import jax.numpy as jnp
from jax import lax
from jax.experimental import pallas as pl
from jax.experimental.pallas import tpu as pltpu
from jax.sharding import PartitionSpec as P

HEAD_DIM = 128
REACH = 4
TILE = 8
PACKED_TILE = 16
NEVER = -1e30
FIELD = 256
VMEM = pl.BlockSpec(memory_space=pltpu.VMEM)
SMEM = pl.BlockSpec(memory_space=pltpu.SMEM)
PARAMS = pltpu.CompilerParams(vmem_limit_bytes=16 * 2**20)


def shifted(value, axis, steps):
    count = lax.axis_size(axis)
    pairs = [(source, (source + steps) % count) for source in range(count)]
    return lax.ppermute(value, axis, pairs)


def slot_plan(owner_ref, length_ref, places_ref, count, capacity):
    myself = lax.axis_index("store")
    seq_count, most_pages = owner_ref.shape
    codes = [[jnp.int32(0)] * capacity for _ in range(REACH)]
    for seq in reversed(range(seq_count)):
        for page in reversed(range(most_pages)):
            gap = owner_ref[seq, page] - myself
            gap = jnp.where(gap < 0, gap + count, gap)
            gap = jnp.where(page < length_ref[seq], gap, jnp.int32(-1))
            code = jnp.int32((FIELD + seq) * FIELD)
            if places_ref is not None:
                code = code + places_ref[seq, page]
            for step in range(REACH):
                mine = gap == step
                slots = codes[step]
                codes[step] = [
                    jnp.where(mine, code if slot == 0 else slots[slot - 1], slots[slot])
                    for slot in range(capacity)
                ]
    return [
        [((code // FIELD) % FIELD, code % FIELD, code // (FIELD * FIELD)) for code in slots]
        for slots in codes
    ]


def spread_rows(queries_ref, rows):
    seq_count = queries_ref.shape[0]
    heads = queries_ref.shape[1] // HEAD_DIM
    for head in range(heads):
        rows[pl.ds(head, seq_count, stride=heads), :] = queries_ref[
            :, head * HEAD_DIM : (head + 1) * HEAD_DIM
        ].astype(jnp.float32)


def slot_rows(rows, seq, heads):
    return rows[pl.ds(pl.multiple_of(seq * heads, TILE), heads), :]


def first_kernel(out_ref):
    out_ref[...] = jnp.zeros_like(out_ref)


def pack_kernel(count, capacity, first_ref, owner_ref, length_ref, places_ref, queries_ref, *refs):
    outs, rows = refs[:-1], refs[-1]
    seq_count, most_pages = owner_ref.shape
    heads = queries_ref.shape[1] // HEAD_DIM
    spread_rows(queries_ref, rows)
    gap = owner_ref[...] - lax.axis_index("store")
    gap = jnp.where(gap < 0, gap + count, gap)
    square = (seq_count, seq_count)
    lengths = jnp.where(
        lax.broadcasted_iota(jnp.int32, square, 0) == lax.broadcasted_iota(jnp.int32, square, 1),
        length_ref[...].reshape(1, seq_count).astype(jnp.float32),
        0.0,
    )
    lengths = jnp.sum(lengths, axis=1, keepdims=True)
    page = lax.broadcasted_iota(jnp.int32, gap.shape, 1)
    entry = lax.broadcasted_iota(jnp.int32, gap.shape, 0) * most_pages + page
    gap = jnp.where(page.astype(jnp.float32) < lengths, gap, -1)
    keys = (entry * FIELD + places_ref[...]).astype(jnp.float32)
    span = float(most_pages * FIELD)
    none = float(seq_count * most_pages * FIELD)
    line = lax.broadcasted_iota(jnp.int32, (PACKED_TILE, HEAD_DIM), 0)
    for step in range(1, REACH):
        out_ref = outs[step - 1]
        left = jnp.where(gap == step, keys, none)
        note = jnp.zeros((PACKED_TILE, HEAD_DIM), jnp.float32)
        for slot in range(capacity):
            key = jnp.min(jnp.min(left, axis=1, keepdims=True), axis=0, keepdims=True)
            left = jnp.where(left > key, left, none)
            value = rows[0:heads, :]
            for seq in range(1, seq_count):
                here = (key >= seq * span) & (key < (seq + 1) * span)
                value = jnp.where(here, rows[seq * heads : (seq + 1) * heads, :], value)
            out_ref[slot * heads : (slot + 1) * heads, :] = value.astype(jnp.bfloat16)
            place = key - jnp.floor(key * (1.0 / FIELD)) * FIELD
            note = jnp.where(line == slot, place, note)
        out_ref[capacity * heads :, :] = note.astype(jnp.bfloat16)


def page_parts(slots, pages_ref, scale):
    kv_count = pages_ref.shape[3] // HEAD_DIM
    group = slots[0][0].shape[0] // kv_count
    scores = [
        jnp.concatenate(
            [
                lax.dot_general(
                    query[kv * group : (kv + 1) * group, :],
                    pages_ref[place, 0, :, kv * HEAD_DIM : (kv + 1) * HEAD_DIM],
                    (((1,), (1,)), ((), ())),
                    preferred_element_type=jnp.float32,
                )
                for kv in range(kv_count)
            ],
            axis=0,
        )
        * scale
        for query, place in slots
    ]
    peaks = [jnp.max(score, axis=1, keepdims=True) for score in scores]
    weights = [jnp.exp(score - peak) for score, peak in zip(scores, peaks)]
    totals = [jnp.sum(weight, axis=1, keepdims=True) for weight in weights]
    sums = []
    for weight, (_, place) in zip(weights, slots):
        high = weight.astype(jnp.bfloat16).astype(jnp.float32)
        low = weight - high
        parts = []
        for kv in range(kv_count):
            mine = slice(kv * group, (kv + 1) * group)
            both = jnp.dot(
                jnp.concatenate([high[mine], low[mine]], axis=0).astype(jnp.bfloat16),
                pages_ref[place, 1, :, kv * HEAD_DIM : (kv + 1) * HEAD_DIM],
                preferred_element_type=jnp.float32,
            )
            parts.append(both[:group] + both[group:])
        sums.append(jnp.concatenate(parts, axis=0))
    return list(zip(peaks, totals, sums))


def to_lanes(column, offset):
    shape = (column.shape[0], HEAD_DIM)
    at = lax.broadcasted_iota(jnp.int32, shape, 0) + offset
    lane = lax.broadcasted_iota(jnp.int32, shape, 1)
    return jnp.where(at == lane, column, 0.0)


def to_column(row, offset, heads):
    shape = (heads, HEAD_DIM)
    at = lax.broadcasted_iota(jnp.int32, shape, 0) + offset
    lane = lax.broadcasted_iota(jnp.int32, shape, 1)
    return jnp.sum(jnp.where(at == lane, row, 0.0), axis=1, keepdims=True)


def attend_kernel(heads, capacity, scale, payload_ref, pages_ref, out_ref):
    notes = payload_ref[capacity * heads :, :].astype(jnp.float32)
    slots = [
        (payload_ref[slot * heads : (slot + 1) * heads, :], notes[slot, 0].astype(jnp.int32))
        for slot in range(capacity)
    ]
    parts = page_parts(slots, pages_ref, scale)
    columns = [part[0] for part in parts] + [part[1] for part in parts]
    lane = lax.broadcasted_iota(jnp.int32, (heads, HEAD_DIM), 1)
    marks = columns[0]
    for at in range(1, 2 * capacity):
        marks = jnp.where(lane >= at * heads, columns[at], marks)
    head = lax.broadcasted_iota(jnp.int32, (heads, HEAD_DIM), 0)
    marks = jnp.where(lax.rem(lane, heads) == head, marks, 0.0)
    row = jnp.sum(marks, axis=0, keepdims=True)
    for slot, part in enumerate(parts):
        out_ref[slot * heads : (slot + 1) * heads, :] = part[2]
    out_ref[capacity * heads :, :] = jnp.broadcast_to(row, (TILE, HEAD_DIM))


def local_kernel(
    count, capacity, scale, owner_ref, length_ref, places_ref, queries_ref, fresh_ref, pages_ref,
    state_ref, bias_ref, rows
):
    seq_count = queries_ref.shape[0]
    heads = queries_ref.shape[1] // HEAD_DIM
    kv_count = fresh_ref.shape[2] // HEAD_DIM
    group = heads // kv_count
    spread_rows(queries_ref, rows)
    plan = slot_plan(owner_ref, length_ref, places_ref, count, capacity)
    local = page_parts(
        [(slot_rows(rows, seq, heads).astype(jnp.bfloat16), place) for seq, place, _ in plan[0]],
        pages_ref,
        scale,
    )
    line = lax.broadcasted_iota(jnp.int32, (TILE, HEAD_DIM), 0)
    lane = lax.broadcasted_iota(jnp.int32, (TILE, HEAD_DIM), 1)
    peaks = jnp.full((TILE, HEAD_DIM), NEVER, jnp.float32)
    totals = jnp.zeros((TILE, HEAD_DIM), jnp.float32)
    for seq in range(seq_count):
        query = rows[seq * heads : (seq + 1) * heads, :]

        def fresh(which):
            new = fresh_ref[seq, which : which + 1, :].astype(jnp.float32)
            return jnp.concatenate(
                [
                    jnp.broadcast_to(new[:, kv * HEAD_DIM : (kv + 1) * HEAD_DIM], (group, HEAD_DIM))
                    for kv in range(kv_count)
                ],
                axis=0,
            )

        own = jnp.sum(query * fresh(0), axis=1, keepdims=True) * scale
        highest = own
        for (at, _, used), (peak, _, _) in zip(plan[0], local):
            highest = jnp.maximum(highest, jnp.where((used > 0) & (at == seq), peak, NEVER))
        own_weight = jnp.exp(own - highest)
        denominator = own_weight
        numerator = own_weight * fresh(1)
        for (at, _, used), (peak, total, summed) in zip(plan[0], local):
            inside = (used > 0) & (at == seq)
            factor = jnp.exp(jnp.where(inside, peak - highest, NEVER))
            denominator = denominator + factor * total
            numerator = numerator + factor * summed
        state_ref[seq * heads : (seq + 1) * heads, :] = numerator
        high_row = jnp.sum(to_lanes(highest, 0), axis=0, keepdims=True)
        total_row = jnp.sum(to_lanes(denominator, 0), axis=0, keepdims=True)
        peaks = jnp.where((line == seq) & (lane < heads), high_row, peaks)
        totals = jnp.where(line == seq, total_row, totals)
    bias_ref[0:TILE, :] = peaks
    for step in range(1, REACH):
        bias = jnp.full((TILE, HEAD_DIM), NEVER, jnp.float32)
        for slot in range(capacity):
            at, _, used = plan[step][slot]
            mine = (line == at) & (lane // heads == slot) & (used > 0)
            bias = jnp.where(mine, 0.0, bias)
        bias_ref[step * TILE : (step + 1) * TILE, :] = bias
    bias_ref[REACH * TILE :, :] = totals


def combine_kernel(seq_count, capacity, state_ref, bias_ref, *refs):
    parts, out_ref, rows = refs[:-2], refs[-2], refs[-1]
    heads = out_ref.shape[1] // HEAD_DIM
    marks = [part[capacity * heads :, :] for part in parts]
    peaks = [bias_ref[0:TILE, :]] + [
        mark + bias_ref[(at + 1) * TILE : (at + 2) * TILE, :] for at, mark in enumerate(marks)
    ]
    totals = [bias_ref[REACH * TILE :, :]] + [
        pltpu.roll(mark, HEAD_DIM - capacity * heads, 1) for mark in marks
    ]

    def over_slots(tile, join):
        whole = tile
        for slot in range(1, capacity):
            whole = join(whole, pltpu.roll(tile, slot * heads, 1))
            whole = join(whole, pltpu.roll(tile, HEAD_DIM - slot * heads, 1))
        return whole

    highest = over_slots(functools.reduce(jnp.maximum, peaks), jnp.maximum)
    factors = [jnp.exp(peak - highest) for peak in peaks]
    share = functools.reduce(jnp.add, [factor * total for factor, total in zip(factors, totals)])
    inverse = 1.0 / over_slots(share, jnp.add)
    for seq in range(seq_count):
        line = slice(seq, seq + 1)
        numerator = to_column(factors[0][line], 0, heads) * state_ref[seq * heads : (seq + 1) * heads, :]
        for factor, part in zip(factors[1:], parts):
            for slot in range(capacity):
                column = to_column(factor[line], slot * heads, heads)
                numerator = numerator + column * part[slot * heads : (slot + 1) * heads, :]
        rows[seq * heads : (seq + 1) * heads, :] = numerator * to_column(inverse[line], 0, heads)
    for head in range(heads):
        out_ref[:, head * HEAD_DIM : (head + 1) * HEAD_DIM] = rows[
            pl.ds(head, seq_count, stride=heads), :
        ].astype(jnp.bfloat16)


def body(queries, new_kv, kv_pages, page_index, page_owner, seq_pages):
    count = lax.axis_size("store")
    seq_count, most_pages = page_index.shape
    capacity = seq_count * most_pages // REACH
    heads = queries.shape[1] // HEAD_DIM
    scale = HEAD_DIM ** (-0.5)
    rows = capacity * heads
    assert kv_pages.shape[0] <= FIELD and seq_count <= TILE
    assert 2 * rows <= HEAD_DIM and heads % TILE == 0
    sent = jax.ShapeDtypeStruct((rows + PACKED_TILE, HEAD_DIM), jnp.bfloat16)
    back = jax.ShapeDtypeStruct((rows + TILE, HEAD_DIM), jnp.float32)
    scratch = [pltpu.VMEM((seq_count * heads, HEAD_DIM), jnp.float32)]
    first = pl.pallas_call(
        first_kernel,
        out_shape=jax.ShapeDtypeStruct((TILE, HEAD_DIM), jnp.float32),
        out_specs=VMEM,
        compiler_params=PARAMS,
        cost_estimate=pl.CostEstimate(flops=2 * 10**9, bytes_accessed=0, transcendentals=0),
        name="first",
    )()
    payloads = pl.pallas_call(
        functools.partial(pack_kernel, count, capacity),
        out_shape=[sent] * (REACH - 1),
        in_specs=[VMEM] * 5,
        out_specs=[VMEM] * (REACH - 1),
        scratch_shapes=scratch,
        compiler_params=PARAMS,
        cost_estimate=pl.CostEstimate(flops=10**12, bytes_accessed=0, transcendentals=0),
        name="pack",
    )(first, page_owner, seq_pages, page_index, queries)
    attend = pl.pallas_call(
        functools.partial(attend_kernel, heads, capacity, scale),
        out_shape=back,
        in_specs=[VMEM] * 2,
        out_specs=VMEM,
        compiler_params=PARAMS,
        name="attend",
    )
    parts = []
    for step in range(1, REACH):
        payload = shifted(payloads[step - 1], "store", step)
        part = attend(payload, kv_pages)
        parts.append(shifted(part, "store", -step))
    state, bias = pl.pallas_call(
        functools.partial(local_kernel, count, capacity, scale),
        out_shape=[
            jax.ShapeDtypeStruct((seq_count * heads, HEAD_DIM), jnp.float32),
            jax.ShapeDtypeStruct(((REACH + 1) * TILE, HEAD_DIM), jnp.float32),
        ],
        in_specs=[SMEM] * 3 + [VMEM] * 3,
        out_specs=[VMEM] * 2,
        scratch_shapes=scratch,
        compiler_params=PARAMS,
        name="local",
    )(page_owner, seq_pages, page_index, queries, new_kv, kv_pages)
    return pl.pallas_call(
        functools.partial(combine_kernel, seq_count, capacity),
        out_shape=jax.ShapeDtypeStruct(queries.shape, queries.dtype),
        in_specs=[VMEM] * (1 + REACH),
        out_specs=VMEM,
        scratch_shapes=scratch,
        compiler_params=PARAMS,
        name="combine",
    )(state, bias, *parts)


def solution(mesh):
    in_specs = (
        P(("groups", "store"), "tensor"),
        P(("groups", "store"), None, "tensor"),
        P(("groups", "store"), None, None, "tensor"),
        P(("groups", "store"), None),
        P(("groups", "store"), None),
        P(("groups", "store")),
    )
    out_specs = P(("groups", "store"), "tensor")

    return jax.shard_map(body, mesh=mesh, in_specs=in_specs, out_specs=out_specs, check_vma=False)
```

```python
import functools

import jax
import jax.numpy as jnp
from jax import lax
from jax.experimental import pallas as pl
from jax.experimental.pallas import tpu as pltpu
from jax.sharding import PartitionSpec as P

HEAD_DIM = 128
REACH = 4
TILE = 8
PACKED_TILE = 16
NEVER = -1e30
FIELD = 256
VMEM = pl.BlockSpec(memory_space=pltpu.VMEM)
SMEM = pl.BlockSpec(memory_space=pltpu.SMEM)
PARAMS = pltpu.CompilerParams(vmem_limit_bytes=16 * 2**20)
BACKS = (1, 3, 2)


def shifted(value, axis, steps):
    count = lax.axis_size(axis)
    pairs = [(source, (source + steps) % count) for source in range(count)]
    return lax.ppermute(value, axis, pairs)


def slot_plan(owner_ref, length_ref, places_ref, count, capacity):
    myself = lax.axis_index("store")
    seq_count, most_pages = owner_ref.shape
    codes = [[jnp.int32(0)] * capacity for _ in range(REACH)]
    for seq in reversed(range(seq_count)):
        for page in reversed(range(most_pages)):
            gap = owner_ref[seq, page] - myself
            gap = jnp.where(gap < 0, gap + count, gap)
            gap = jnp.where(page < length_ref[seq], gap, jnp.int32(-1))
            code = jnp.int32((FIELD + seq) * FIELD)
            if places_ref is not None:
                code = code + places_ref[seq, page]
            for step in range(REACH):
                mine = gap == step
                slots = codes[step]
                codes[step] = [
                    jnp.where(mine, code if slot == 0 else slots[slot - 1], slots[slot])
                    for slot in range(capacity)
                ]
    return [
        [((code // FIELD) % FIELD, code % FIELD, code // (FIELD * FIELD)) for code in slots]
        for slots in codes
    ]


def spread_rows(queries_ref, rows):
    seq_count = queries_ref.shape[0]
    heads = queries_ref.shape[1] // HEAD_DIM
    for head in range(heads):
        rows[pl.ds(head, seq_count, stride=heads), :] = queries_ref[
            :, head * HEAD_DIM : (head + 1) * HEAD_DIM
        ].astype(jnp.float32)


def slot_rows(rows, seq, heads):
    return rows[pl.ds(pl.multiple_of(seq * heads, TILE), heads), :]


def first_kernel(out_ref):
    out_ref[...] = jnp.zeros_like(out_ref)


def pack_kernel(count, capacity, first_ref, owner_ref, length_ref, places_ref, queries_ref, *refs):
    outs, rows = refs[:-1], refs[-1]
    seq_count, most_pages = owner_ref.shape
    heads = queries_ref.shape[1] // HEAD_DIM
    spread_rows(queries_ref, rows)
    gap = owner_ref[...] - lax.axis_index("store")
    gap = jnp.where(gap < 0, gap + count, gap)
    square = (seq_count, seq_count)
    lengths = jnp.where(
        lax.broadcasted_iota(jnp.int32, square, 0) == lax.broadcasted_iota(jnp.int32, square, 1),
        length_ref[...].reshape(1, seq_count).astype(jnp.float32),
        0.0,
    )
    lengths = jnp.sum(lengths, axis=1, keepdims=True)
    page = lax.broadcasted_iota(jnp.int32, gap.shape, 1)
    entry = lax.broadcasted_iota(jnp.int32, gap.shape, 0) * most_pages + page
    gap = jnp.where(page.astype(jnp.float32) < lengths, gap, -1)
    keys = (entry * FIELD + places_ref[...]).astype(jnp.float32)
    span = float(most_pages * FIELD)
    none = float(seq_count * most_pages * FIELD)
    line = lax.broadcasted_iota(jnp.int32, (PACKED_TILE, HEAD_DIM), 0)
    for step in range(1, REACH):
        out_ref = outs[step - 1]
        left = jnp.where(gap == step, keys, none)
        note = jnp.zeros((PACKED_TILE, HEAD_DIM), jnp.float32)
        for slot in range(capacity):
            key = jnp.min(jnp.min(left, axis=1, keepdims=True), axis=0, keepdims=True)
            left = jnp.where(left > key, left, none)
            value = rows[0:heads, :]
            for seq in range(1, seq_count):
                here = (key >= seq * span) & (key < (seq + 1) * span)
                value = jnp.where(here, rows[seq * heads : (seq + 1) * heads, :], value)
            out_ref[slot * heads : (slot + 1) * heads, :] = value.astype(jnp.bfloat16)
            place = key - jnp.floor(key * (1.0 / FIELD)) * FIELD
            note = jnp.where(line == slot, place, note)
        out_ref[capacity * heads :, :] = note.astype(jnp.bfloat16)


def page_parts(slots, pages_ref, scale):
    kv_count = pages_ref.shape[3] // HEAD_DIM
    group = slots[0][0].shape[0] // kv_count
    scores = [
        jnp.concatenate(
            [
                lax.dot_general(
                    query[kv * group : (kv + 1) * group, :],
                    pages_ref[place, 0, :, kv * HEAD_DIM : (kv + 1) * HEAD_DIM],
                    (((1,), (1,)), ((), ())),
                    preferred_element_type=jnp.float32,
                )
                for kv in range(kv_count)
            ],
            axis=0,
        )
        * scale
        for query, place in slots
    ]
    peaks = [jnp.max(score, axis=1, keepdims=True) for score in scores]
    weights = [jnp.exp(score - peak) for score, peak in zip(scores, peaks)]
    totals = [jnp.sum(weight, axis=1, keepdims=True) for weight in weights]
    sums = []
    for weight, (_, place) in zip(weights, slots):
        high = weight.astype(jnp.bfloat16).astype(jnp.float32)
        low = weight - high
        parts = []
        for kv in range(kv_count):
            mine = slice(kv * group, (kv + 1) * group)
            both = jnp.dot(
                jnp.concatenate([high[mine], low[mine]], axis=0).astype(jnp.bfloat16),
                pages_ref[place, 1, :, kv * HEAD_DIM : (kv + 1) * HEAD_DIM],
                preferred_element_type=jnp.float32,
            )
            parts.append(both[:group] + both[group:])
        sums.append(jnp.concatenate(parts, axis=0))
    return list(zip(peaks, totals, sums))


def to_lanes(column, offset):
    shape = (column.shape[0], HEAD_DIM)
    at = lax.broadcasted_iota(jnp.int32, shape, 0) + offset
    lane = lax.broadcasted_iota(jnp.int32, shape, 1)
    return jnp.where(at == lane, column, 0.0)


def to_column(row, offset, heads):
    shape = (heads, HEAD_DIM)
    at = lax.broadcasted_iota(jnp.int32, shape, 0) + offset
    lane = lax.broadcasted_iota(jnp.int32, shape, 1)
    return jnp.sum(jnp.where(at == lane, row, 0.0), axis=1, keepdims=True)


def attend_kernel(heads, capacity, scale, payload_ref, pages_ref, out_ref):
    notes = payload_ref[capacity * heads :, :].astype(jnp.float32)
    slots = [
        (payload_ref[slot * heads : (slot + 1) * heads, :], notes[slot, 0].astype(jnp.int32))
        for slot in range(capacity)
    ]
    parts = page_parts(slots, pages_ref, scale)
    columns = [part[0] for part in parts] + [part[1] for part in parts]
    lane = lax.broadcasted_iota(jnp.int32, (heads, HEAD_DIM), 1)
    marks = columns[0]
    for at in range(1, 2 * capacity):
        marks = jnp.where(lane >= at * heads, columns[at], marks)
    head = lax.broadcasted_iota(jnp.int32, (heads, HEAD_DIM), 0)
    marks = jnp.where(lax.rem(lane, heads) == head, marks, 0.0)
    row = jnp.sum(marks, axis=0, keepdims=True)
    for slot, part in enumerate(parts):
        out_ref[slot * heads : (slot + 1) * heads, :] = part[2]
    out_ref[capacity * heads :, :] = jnp.broadcast_to(row, (TILE, HEAD_DIM))


def local_kernel(
    count, capacity, scale, owner_ref, length_ref, places_ref, queries_ref, fresh_ref, pages_ref,
    part_ref, state_ref, bias_ref, rows
):
    seq_count = queries_ref.shape[0]
    heads = queries_ref.shape[1] // HEAD_DIM
    kv_count = fresh_ref.shape[2] // HEAD_DIM
    group = heads // kv_count
    spread_rows(queries_ref, rows)
    plan = slot_plan(owner_ref, length_ref, places_ref, count, capacity)
    local = page_parts(
        [(slot_rows(rows, seq, heads).astype(jnp.bfloat16), place) for seq, place, _ in plan[0]],
        pages_ref,
        scale,
    )
    marks = part_ref[capacity * heads : capacity * heads + 1, :]
    local += [
        (
            to_column(marks, slot * heads, heads),
            to_column(marks, (capacity + slot) * heads, heads),
            part_ref[slot * heads : (slot + 1) * heads, :],
        )
        for slot in range(capacity)
    ]
    held = plan[0] + plan[BACKS[0]]
    line = lax.broadcasted_iota(jnp.int32, (TILE, HEAD_DIM), 0)
    lane = lax.broadcasted_iota(jnp.int32, (TILE, HEAD_DIM), 1)
    peaks = jnp.full((TILE, HEAD_DIM), NEVER, jnp.float32)
    totals = jnp.zeros((TILE, HEAD_DIM), jnp.float32)
    for seq in range(seq_count):
        query = rows[seq * heads : (seq + 1) * heads, :]

        def fresh(which):
            new = fresh_ref[seq, which : which + 1, :].astype(jnp.float32)
            return jnp.concatenate(
                [
                    jnp.broadcast_to(new[:, kv * HEAD_DIM : (kv + 1) * HEAD_DIM], (group, HEAD_DIM))
                    for kv in range(kv_count)
                ],
                axis=0,
            )

        own = jnp.sum(query * fresh(0), axis=1, keepdims=True) * scale
        highest = own
        for (at, _, used), (peak, _, _) in zip(held, local):
            highest = jnp.maximum(highest, jnp.where((used > 0) & (at == seq), peak, NEVER))
        own_weight = jnp.exp(own - highest)
        denominator = own_weight
        numerator = own_weight * fresh(1)
        for (at, _, used), (peak, total, summed) in zip(held, local):
            inside = (used > 0) & (at == seq)
            factor = jnp.exp(jnp.where(inside, peak - highest, NEVER))
            denominator = denominator + factor * total
            numerator = numerator + factor * summed
        state_ref[seq * heads : (seq + 1) * heads, :] = numerator
        high_row = jnp.sum(to_lanes(highest, 0), axis=0, keepdims=True)
        total_row = jnp.sum(to_lanes(denominator, 0), axis=0, keepdims=True)
        peaks = jnp.where((line == seq) & (lane < heads), high_row, peaks)
        totals = jnp.where(line == seq, total_row, totals)
    bias_ref[0:TILE, :] = peaks
    for tile, step in enumerate(BACKS[1:], 1):
        bias = jnp.full((TILE, HEAD_DIM), NEVER, jnp.float32)
        for slot in range(capacity):
            at, _, used = plan[step][slot]
            mine = (line == at) & (lane // heads == slot) & (used > 0)
            bias = jnp.where(mine, 0.0, bias)
        bias_ref[tile * TILE : (tile + 1) * TILE, :] = bias
    bias_ref[(REACH - 1) * TILE :, :] = totals


def combine_kernel(seq_count, capacity, state_ref, bias_ref, *refs):
    parts, out_ref, rows = refs[:-2], refs[-2], refs[-1]
    heads = out_ref.shape[1] // HEAD_DIM
    marks = [part[capacity * heads :, :] for part in parts]
    peaks = [bias_ref[0:TILE, :]] + [
        mark + bias_ref[(at + 1) * TILE : (at + 2) * TILE, :] for at, mark in enumerate(marks)
    ]
    totals = [bias_ref[(REACH - 1) * TILE :, :]] + [
        pltpu.roll(mark, HEAD_DIM - capacity * heads, 1) for mark in marks
    ]

    def over_slots(tile, join):
        whole = tile
        for slot in range(1, capacity):
            whole = join(whole, pltpu.roll(tile, slot * heads, 1))
            whole = join(whole, pltpu.roll(tile, HEAD_DIM - slot * heads, 1))
        return whole

    highest = over_slots(functools.reduce(jnp.maximum, peaks), jnp.maximum)
    factors = [jnp.exp(peak - highest) for peak in peaks]
    share = functools.reduce(jnp.add, [factor * total for factor, total in zip(factors, totals)])
    inverse = 1.0 / over_slots(share, jnp.add)
    factors = [factor * inverse for factor in factors]
    for seq in range(seq_count):
        line = slice(seq, seq + 1)
        numerator = to_column(factors[0][line], 0, heads) * state_ref[seq * heads : (seq + 1) * heads, :]
        for factor, part in zip(factors[1:], parts):
            for slot in range(capacity):
                column = to_column(factor[line], slot * heads, heads)
                numerator = numerator + column * part[slot * heads : (slot + 1) * heads, :]
        rows[seq * heads : (seq + 1) * heads, :] = numerator
    for head in range(heads):
        out_ref[:, head * HEAD_DIM : (head + 1) * HEAD_DIM] = rows[
            pl.ds(head, seq_count, stride=heads), :
        ].astype(jnp.bfloat16)


def body(queries, new_kv, kv_pages, page_index, page_owner, seq_pages):
    count = lax.axis_size("store")
    seq_count, most_pages = page_index.shape
    capacity = seq_count * most_pages // REACH
    heads = queries.shape[1] // HEAD_DIM
    scale = HEAD_DIM ** (-0.5)
    rows = capacity * heads
    assert kv_pages.shape[0] <= FIELD and seq_count <= TILE
    assert 2 * rows <= HEAD_DIM and heads % TILE == 0
    sent = jax.ShapeDtypeStruct((rows + PACKED_TILE, HEAD_DIM), jnp.bfloat16)
    back = jax.ShapeDtypeStruct((rows + TILE, HEAD_DIM), jnp.float32)
    scratch = [pltpu.VMEM((seq_count * heads, HEAD_DIM), jnp.float32)]
    first = pl.pallas_call(
        first_kernel,
        out_shape=jax.ShapeDtypeStruct((TILE, HEAD_DIM), jnp.float32),
        out_specs=VMEM,
        compiler_params=PARAMS,
        cost_estimate=pl.CostEstimate(flops=2 * 10**9, bytes_accessed=0, transcendentals=0),
        name="first",
    )()
    payloads = pl.pallas_call(
        functools.partial(pack_kernel, count, capacity),
        out_shape=[sent] * (REACH - 1),
        in_specs=[VMEM] * 5,
        out_specs=[VMEM] * (REACH - 1),
        scratch_shapes=scratch,
        compiler_params=PARAMS,
        cost_estimate=pl.CostEstimate(flops=10**12, bytes_accessed=0, transcendentals=0),
        name="pack",
    )(first, page_owner, seq_pages, page_index, queries)
    attend = pl.pallas_call(
        functools.partial(attend_kernel, heads, capacity, scale),
        out_shape=back,
        in_specs=[VMEM] * 2,
        out_specs=VMEM,
        compiler_params=PARAMS,
        name="attend",
    )
    parts = {}
    for step in range(1, REACH):
        payload = shifted(payloads[step - 1], "store", step)
        part = attend(payload, kv_pages)
        parts[step] = shifted(part, "store", -step)
    state, bias = pl.pallas_call(
        functools.partial(local_kernel, count, capacity, scale),
        out_shape=[
            jax.ShapeDtypeStruct((seq_count * heads, HEAD_DIM), jnp.float32),
            jax.ShapeDtypeStruct((REACH * TILE, HEAD_DIM), jnp.float32),
        ],
        in_specs=[SMEM] * 3 + [VMEM] * 4,
        out_specs=[VMEM] * 2,
        scratch_shapes=scratch,
        compiler_params=PARAMS,
        name="local",
    )(page_owner, seq_pages, page_index, queries, new_kv, kv_pages, parts[BACKS[0]])
    return pl.pallas_call(
        functools.partial(combine_kernel, seq_count, capacity),
        out_shape=jax.ShapeDtypeStruct(queries.shape, queries.dtype),
        in_specs=[VMEM] * REACH,
        out_specs=VMEM,
        scratch_shapes=scratch,
        compiler_params=PARAMS,
        name="combine",
    )(state, bias, *[parts[step] for step in BACKS[1:]])


def solution(mesh):
    in_specs = (
        P(("groups", "store"), "tensor"),
        P(("groups", "store"), None, "tensor"),
        P(("groups", "store"), None, None, "tensor"),
        P(("groups", "store"), None),
        P(("groups", "store"), None),
        P(("groups", "store")),
    )
    out_specs = P(("groups", "store"), "tensor")

    return jax.shard_map(body, mesh=mesh, in_specs=in_specs, out_specs=out_specs, check_vma=False)
```

```python
import functools

import jax
import jax.numpy as jnp
from jax import lax
from jax.experimental import pallas as pl
from jax.experimental.pallas import tpu as pltpu
from jax.sharding import PartitionSpec as P

HEAD_DIM = 128
REACH = 4
TILE = 8
PACKED_TILE = 8
NEVER = -1e30
FIELD = 256
VMEM = pl.BlockSpec(memory_space=pltpu.VMEM)
SMEM = pl.BlockSpec(memory_space=pltpu.SMEM)
PARAMS = pltpu.CompilerParams(vmem_limit_bytes=16 * 2**20)


def shifted(value, axis, steps):
    count = lax.axis_size(axis)
    pairs = [(source, (source + steps) % count) for source in range(count)]
    return lax.ppermute(value, axis, pairs)


def slot_plan(owner_ref, length_ref, places_ref, count, capacity):
    myself = lax.axis_index("store")
    seq_count, most_pages = owner_ref.shape
    codes = [[jnp.int32(0)] * capacity for _ in range(REACH)]
    for seq in reversed(range(seq_count)):
        for page in reversed(range(most_pages)):
            gap = owner_ref[seq, page] - myself
            gap = jnp.where(gap < 0, gap + count, gap)
            gap = jnp.where(page < length_ref[seq], gap, jnp.int32(-1))
            code = jnp.int32((FIELD + seq) * FIELD)
            if places_ref is not None:
                code = code + places_ref[seq, page]
            for step in range(REACH):
                mine = gap == step
                slots = codes[step]
                codes[step] = [
                    jnp.where(mine, code if slot == 0 else slots[slot - 1], slots[slot])
                    for slot in range(capacity)
                ]
    return [
        [((code // FIELD) % FIELD, code % FIELD, code // (FIELD * FIELD)) for code in slots]
        for slots in codes
    ]


def spread_rows(queries_ref, rows):
    seq_count = queries_ref.shape[0]
    heads = queries_ref.shape[1] // HEAD_DIM
    for head in range(heads):
        rows[pl.ds(head, seq_count, stride=heads), :] = queries_ref[
            :, head * HEAD_DIM : (head + 1) * HEAD_DIM
        ].astype(jnp.float32)


def slot_rows(rows, seq, heads):
    return rows[pl.ds(pl.multiple_of(seq * heads, TILE), heads), :]


def first_kernel(out_ref):
    out_ref[...] = jnp.zeros_like(out_ref)


def pack_kernel(count, capacity, first_ref, owner_ref, length_ref, places_ref, queries_ref, *refs):
    outs, rows = refs[:-1], refs[-1]
    seq_count, most_pages = owner_ref.shape
    heads = queries_ref.shape[1] // HEAD_DIM
    spread_rows(queries_ref, rows)
    gap = owner_ref[...] - lax.axis_index("store")
    gap = jnp.where(gap < 0, gap + count, gap)
    square = (seq_count, seq_count)
    lengths = jnp.where(
        lax.broadcasted_iota(jnp.int32, square, 0) == lax.broadcasted_iota(jnp.int32, square, 1),
        length_ref[...].reshape(1, seq_count).astype(jnp.float32),
        0.0,
    )
    lengths = jnp.sum(lengths, axis=1, keepdims=True)
    page = lax.broadcasted_iota(jnp.int32, gap.shape, 1)
    entry = lax.broadcasted_iota(jnp.int32, gap.shape, 0) * most_pages + page
    gap = jnp.where(page.astype(jnp.float32) < lengths, gap, -1)
    keys = (entry * FIELD + places_ref[...]).astype(jnp.float32)
    span = float(most_pages * FIELD)
    none = float(seq_count * most_pages * FIELD)
    line = lax.broadcasted_iota(jnp.int32, (PACKED_TILE, HEAD_DIM), 0)
    for step in range(1, REACH):
        out_ref = outs[step - 1]
        left = jnp.where(gap == step, keys, none)
        note = jnp.zeros((PACKED_TILE, HEAD_DIM), jnp.float32)
        for slot in range(capacity):
            key = jnp.min(jnp.min(left, axis=1, keepdims=True), axis=0, keepdims=True)
            left = jnp.where(left > key, left, none)
            value = rows[0:heads, :]
            for seq in range(1, seq_count):
                here = (key >= seq * span) & (key < (seq + 1) * span)
                value = jnp.where(here, rows[seq * heads : (seq + 1) * heads, :], value)
            out_ref[slot * heads : (slot + 1) * heads, :] = value.astype(jnp.bfloat16)
            place = key - jnp.floor(key * (1.0 / FIELD)) * FIELD
            note = jnp.where(line == slot, place, note)
        out_ref[capacity * heads :, :] = note.astype(jnp.bfloat16)


def page_parts(slots, pages_ref, scale):
    kv_count = pages_ref.shape[3] // HEAD_DIM
    group = slots[0][0].shape[0] // kv_count
    scores = [
        jnp.concatenate(
            [
                lax.dot_general(
                    query[kv * group : (kv + 1) * group, :],
                    pages_ref[place, 0, :, kv * HEAD_DIM : (kv + 1) * HEAD_DIM],
                    (((1,), (1,)), ((), ())),
                    preferred_element_type=jnp.float32,
                )
                for kv in range(kv_count)
            ],
            axis=0,
        )
        * scale
        for query, place in slots
    ]
    peaks = [jnp.max(score, axis=1, keepdims=True) for score in scores]
    weights = [jnp.exp(score - peak) for score, peak in zip(scores, peaks)]
    totals = [jnp.sum(weight, axis=1, keepdims=True) for weight in weights]
    sums = []
    for weight, (_, place) in zip(weights, slots):
        high = weight.astype(jnp.bfloat16).astype(jnp.float32)
        low = weight - high
        parts = []
        for kv in range(kv_count):
            mine = slice(kv * group, (kv + 1) * group)
            both = jnp.dot(
                jnp.concatenate([high[mine], low[mine]], axis=0).astype(jnp.bfloat16),
                pages_ref[place, 1, :, kv * HEAD_DIM : (kv + 1) * HEAD_DIM],
                preferred_element_type=jnp.float32,
            )
            parts.append(both[:group] + both[group:])
        sums.append(jnp.concatenate(parts, axis=0))
    return list(zip(peaks, totals, sums))


def to_lanes(column, offset):
    shape = (column.shape[0], HEAD_DIM)
    at = lax.broadcasted_iota(jnp.int32, shape, 0) + offset
    lane = lax.broadcasted_iota(jnp.int32, shape, 1)
    return jnp.where(at == lane, column, 0.0)


def to_column(row, offset, heads):
    shape = (heads, HEAD_DIM)
    at = lax.broadcasted_iota(jnp.int32, shape, 0) + offset
    lane = lax.broadcasted_iota(jnp.int32, shape, 1)
    return jnp.sum(jnp.where(at == lane, row, 0.0), axis=1, keepdims=True)


def attend_kernel(heads, capacity, scale, payload_ref, pages_ref, out_ref):
    notes = payload_ref[capacity * heads :, :].astype(jnp.float32)
    slots = [
        (payload_ref[slot * heads : (slot + 1) * heads, :], notes[slot, 0].astype(jnp.int32))
        for slot in range(capacity)
    ]
    marks = jnp.zeros((heads, HEAD_DIM), jnp.float32)
    for slot, (peak, total, summed) in enumerate(page_parts(slots, pages_ref, scale)):
        out_ref[slot * heads : (slot + 1) * heads, :] = summed
        marks = marks + to_lanes(peak, slot * heads) + to_lanes(total, (capacity + slot) * heads)
    row = jnp.sum(marks, axis=0, keepdims=True)
    out_ref[capacity * heads :, :] = jnp.broadcast_to(row, (TILE, HEAD_DIM))


def local_kernel(
    count, capacity, scale, owner_ref, length_ref, places_ref, queries_ref, fresh_ref, pages_ref,
    state_ref, bias_ref, rows
):
    seq_count = queries_ref.shape[0]
    heads = queries_ref.shape[1] // HEAD_DIM
    kv_count = fresh_ref.shape[2] // HEAD_DIM
    group = heads // kv_count
    spread_rows(queries_ref, rows)
    plan = slot_plan(owner_ref, length_ref, places_ref, count, capacity)
    local = page_parts(
        [(slot_rows(rows, seq, heads).astype(jnp.bfloat16), place) for seq, place, _ in plan[0]],
        pages_ref,
        scale,
    )
    line = lax.broadcasted_iota(jnp.int32, (TILE, HEAD_DIM), 0)
    lane = lax.broadcasted_iota(jnp.int32, (TILE, HEAD_DIM), 1)
    peaks = jnp.full((TILE, HEAD_DIM), NEVER, jnp.float32)
    totals = jnp.zeros((TILE, HEAD_DIM), jnp.float32)
    for seq in range(seq_count):
        query = rows[seq * heads : (seq + 1) * heads, :]

        def fresh(which):
            new = fresh_ref[seq, which : which + 1, :].astype(jnp.float32)
            return jnp.concatenate(
                [
                    jnp.broadcast_to(new[:, kv * HEAD_DIM : (kv + 1) * HEAD_DIM], (group, HEAD_DIM))
                    for kv in range(kv_count)
                ],
                axis=0,
            )

        own = jnp.sum(query * fresh(0), axis=1, keepdims=True) * scale
        highest = own
        for (at, _, used), (peak, _, _) in zip(plan[0], local):
            highest = jnp.maximum(highest, jnp.where((used > 0) & (at == seq), peak, NEVER))
        own_weight = jnp.exp(own - highest)
        denominator = own_weight
        numerator = own_weight * fresh(1)
        for (at, _, used), (peak, total, summed) in zip(plan[0], local):
            inside = (used > 0) & (at == seq)
            factor = jnp.exp(jnp.where(inside, peak - highest, NEVER))
            denominator = denominator + factor * total
            numerator = numerator + factor * summed
        state_ref[seq * heads : (seq + 1) * heads, :] = numerator
        high_row = jnp.sum(to_lanes(highest, 0), axis=0, keepdims=True)
        total_row = jnp.sum(to_lanes(denominator, 0), axis=0, keepdims=True)
        peaks = jnp.where((line == seq) & (lane < heads), high_row, peaks)
        totals = jnp.where(line == seq, total_row, totals)
    bias_ref[0:TILE, :] = peaks
    for step in range(1, REACH):
        bias = jnp.full((TILE, HEAD_DIM), NEVER, jnp.float32)
        for slot in range(capacity):
            at, _, used = plan[step][slot]
            mine = (line == at) & (lane // heads == slot) & (used > 0)
            bias = jnp.where(mine, 0.0, bias)
        bias_ref[step * TILE : (step + 1) * TILE, :] = bias
    bias_ref[REACH * TILE :, :] = totals


def combine_kernel(seq_count, capacity, state_ref, bias_ref, *refs):
    parts, out_ref, rows = refs[:-2], refs[-2], refs[-1]
    heads = out_ref.shape[1] // HEAD_DIM
    marks = [part[capacity * heads :, :] for part in parts]
    peaks = [bias_ref[0:TILE, :]] + [
        mark + bias_ref[(at + 1) * TILE : (at + 2) * TILE, :] for at, mark in enumerate(marks)
    ]
    totals = [bias_ref[REACH * TILE :, :]] + [
        pltpu.roll(mark, HEAD_DIM - capacity * heads, 1) for mark in marks
    ]

    def over_slots(tile, join):
        whole = tile
        for slot in range(1, capacity):
            whole = join(whole, pltpu.roll(tile, slot * heads, 1))
            whole = join(whole, pltpu.roll(tile, HEAD_DIM - slot * heads, 1))
        return whole

    highest = over_slots(functools.reduce(jnp.maximum, peaks), jnp.maximum)
    factors = [jnp.exp(peak - highest) for peak in peaks]
    share = functools.reduce(jnp.add, [factor * total for factor, total in zip(factors, totals)])
    inverse = 1.0 / over_slots(share, jnp.add)
    factors = [factor * inverse for factor in factors]
    for seq in range(seq_count):
        line = slice(seq, seq + 1)
        numerator = to_column(factors[0][line], 0, heads) * state_ref[seq * heads : (seq + 1) * heads, :]
        for factor, part in zip(factors[1:], parts):
            for slot in range(capacity):
                column = to_column(factor[line], slot * heads, heads)
                numerator = numerator + column * part[slot * heads : (slot + 1) * heads, :]
        rows[seq * heads : (seq + 1) * heads, :] = numerator
    for head in range(heads):
        out_ref[:, head * HEAD_DIM : (head + 1) * HEAD_DIM] = rows[
            pl.ds(head, seq_count, stride=heads), :
        ].astype(jnp.bfloat16)


def body(queries, new_kv, kv_pages, page_index, page_owner, seq_pages):
    count = lax.axis_size("store")
    seq_count, most_pages = page_index.shape
    capacity = seq_count * most_pages // REACH
    heads = queries.shape[1] // HEAD_DIM
    scale = HEAD_DIM ** (-0.5)
    rows = capacity * heads
    assert kv_pages.shape[0] <= FIELD and seq_count <= TILE
    assert 2 * rows <= HEAD_DIM and heads % TILE == 0
    sent = jax.ShapeDtypeStruct((rows + PACKED_TILE, HEAD_DIM), jnp.bfloat16)
    back = jax.ShapeDtypeStruct((rows + TILE, HEAD_DIM), jnp.float32)
    scratch = [pltpu.VMEM((seq_count * heads, HEAD_DIM), jnp.float32)]
    first = pl.pallas_call(
        first_kernel,
        out_shape=jax.ShapeDtypeStruct((TILE, HEAD_DIM), jnp.float32),
        out_specs=VMEM,
        compiler_params=PARAMS,
        cost_estimate=pl.CostEstimate(flops=2 * 10**9, bytes_accessed=0, transcendentals=0),
        name="first",
    )()
    payloads = pl.pallas_call(
        functools.partial(pack_kernel, count, capacity),
        out_shape=[sent] * (REACH - 1),
        in_specs=[VMEM] * 5,
        out_specs=[VMEM] * (REACH - 1),
        scratch_shapes=scratch,
        compiler_params=PARAMS,
        cost_estimate=pl.CostEstimate(flops=10**12, bytes_accessed=0, transcendentals=0),
        name="pack",
    )(first, page_owner, seq_pages, page_index, queries)
    attend = pl.pallas_call(
        functools.partial(attend_kernel, heads, capacity, scale),
        out_shape=back,
        in_specs=[VMEM] * 2,
        out_specs=VMEM,
        compiler_params=PARAMS,
        name="attend",
    )
    parts = []
    for step in range(1, REACH):
        payload = shifted(payloads[step - 1], "store", step)
        part = attend(payload, kv_pages)
        parts.append(shifted(part, "store", -step))
    state, bias = pl.pallas_call(
        functools.partial(local_kernel, count, capacity, scale),
        out_shape=[
            jax.ShapeDtypeStruct((seq_count * heads, HEAD_DIM), jnp.float32),
            jax.ShapeDtypeStruct(((REACH + 1) * TILE, HEAD_DIM), jnp.float32),
        ],
        in_specs=[SMEM] * 3 + [VMEM] * 3,
        out_specs=[VMEM] * 2,
        scratch_shapes=scratch,
        compiler_params=PARAMS,
        name="local",
    )(page_owner, seq_pages, page_index, queries, new_kv, kv_pages)
    return pl.pallas_call(
        functools.partial(combine_kernel, seq_count, capacity),
        out_shape=jax.ShapeDtypeStruct(queries.shape, queries.dtype),
        in_specs=[VMEM] * (1 + REACH),
        out_specs=VMEM,
        scratch_shapes=scratch,
        compiler_params=PARAMS,
        name="combine",
    )(state, bias, *parts)


def solution(mesh):
    in_specs = (
        P(("groups", "store"), "tensor"),
        P(("groups", "store"), None, "tensor"),
        P(("groups", "store"), None, None, "tensor"),
        P(("groups", "store"), None),
        P(("groups", "store"), None),
        P(("groups", "store")),
    )
    out_specs = P(("groups", "store"), "tensor")

    return jax.shard_map(body, mesh=mesh, in_specs=in_specs, out_specs=out_specs, check_vma=False)
```

```python
import functools

import jax
import jax.numpy as jnp
from jax import lax
from jax.experimental import pallas as pl
from jax.experimental.pallas import tpu as pltpu
from jax.sharding import PartitionSpec as P

HEAD_DIM = 128
REACH = 4
TILE = 8
PACKED_TILE = 8
NEVER = -1e30
FIELD = 256
VMEM = pl.BlockSpec(memory_space=pltpu.VMEM)
SMEM = pl.BlockSpec(memory_space=pltpu.SMEM)
PARAMS = pltpu.CompilerParams(vmem_limit_bytes=16 * 2**20)


def shifted(value, axis, steps):
    count = lax.axis_size(axis)
    pairs = [(source, (source + steps) % count) for source in range(count)]
    return lax.ppermute(value, axis, pairs)


def slot_plan(owner_ref, length_ref, places_ref, count, capacity):
    myself = lax.axis_index("store")
    seq_count, most_pages = owner_ref.shape
    codes = [[jnp.int32(0)] * capacity for _ in range(REACH)]
    for seq in reversed(range(seq_count)):
        for page in reversed(range(most_pages)):
            gap = owner_ref[seq, page] - myself
            gap = jnp.where(gap < 0, gap + count, gap)
            gap = jnp.where(page < length_ref[seq], gap, jnp.int32(-1))
            code = jnp.int32((FIELD + seq) * FIELD)
            if places_ref is not None:
                code = code + places_ref[seq, page]
            for step in range(REACH):
                mine = gap == step
                slots = codes[step]
                codes[step] = [
                    jnp.where(mine, code if slot == 0 else slots[slot - 1], slots[slot])
                    for slot in range(capacity)
                ]
    return [
        [((code // FIELD) % FIELD, code % FIELD, code // (FIELD * FIELD)) for code in slots]
        for slots in codes
    ]


def spread_rows(queries_ref, rows):
    seq_count = queries_ref.shape[0]
    heads = queries_ref.shape[1] // HEAD_DIM
    for head in range(heads):
        rows[pl.ds(head, seq_count, stride=heads), :] = queries_ref[
            :, head * HEAD_DIM : (head + 1) * HEAD_DIM
        ].astype(jnp.float32)


def slot_rows(rows, seq, heads):
    return rows[pl.ds(pl.multiple_of(seq * heads, TILE), heads), :]


def first_kernel(out_ref):
    out_ref[...] = jnp.zeros_like(out_ref)


def pack_kernel(count, capacity, first_ref, owner_ref, length_ref, places_ref, queries_ref, *refs):
    outs, rows = refs[:-1], refs[-1]
    seq_count, most_pages = owner_ref.shape
    heads = queries_ref.shape[1] // HEAD_DIM
    spread_rows(queries_ref, rows)
    gap = owner_ref[...] - lax.axis_index("store")
    gap = jnp.where(gap < 0, gap + count, gap)
    square = (seq_count, seq_count)
    lengths = jnp.where(
        lax.broadcasted_iota(jnp.int32, square, 0) == lax.broadcasted_iota(jnp.int32, square, 1),
        length_ref[...].reshape(1, seq_count).astype(jnp.float32),
        0.0,
    )
    lengths = jnp.sum(lengths, axis=1, keepdims=True)
    page = lax.broadcasted_iota(jnp.int32, gap.shape, 1)
    entry = lax.broadcasted_iota(jnp.int32, gap.shape, 0) * most_pages + page
    gap = jnp.where(page.astype(jnp.float32) < lengths, gap, -1)
    keys = (entry * FIELD + places_ref[...]).astype(jnp.float32)
    span = float(most_pages * FIELD)
    none = float(seq_count * most_pages * FIELD)
    line = lax.broadcasted_iota(jnp.int32, (PACKED_TILE, HEAD_DIM), 0)
    for step in range(1, REACH):
        out_ref = outs[step - 1]
        left = jnp.where(gap == step, keys, none)
        note = jnp.zeros((PACKED_TILE, HEAD_DIM), jnp.float32)
        for slot in range(capacity):
            key = jnp.min(jnp.min(left, axis=1, keepdims=True), axis=0, keepdims=True)
            left = jnp.where(left > key, left, none)
            value = rows[0:heads, :]
            for seq in range(1, seq_count):
                here = (key >= seq * span) & (key < (seq + 1) * span)
                value = jnp.where(here, rows[seq * heads : (seq + 1) * heads, :], value)
            out_ref[slot * heads : (slot + 1) * heads, :] = value.astype(jnp.bfloat16)
            place = key - jnp.floor(key * (1.0 / FIELD)) * FIELD
            note = jnp.where(line == slot, place, note)
        out_ref[capacity * heads :, :] = note.astype(jnp.bfloat16)


def page_parts(slots, pages_ref, scale):
    kv_count = pages_ref.shape[3] // HEAD_DIM
    group = slots[0][0].shape[0] // kv_count
    scores = [
        jnp.concatenate(
            [
                lax.dot_general(
                    query[kv * group : (kv + 1) * group, :],
                    pages_ref[place, 0, :, kv * HEAD_DIM : (kv + 1) * HEAD_DIM],
                    (((1,), (1,)), ((), ())),
                    preferred_element_type=jnp.float32,
                )
                for kv in range(kv_count)
            ],
            axis=0,
        )
        * scale
        for query, place in slots
    ]
    peaks = [jnp.max(score, axis=1, keepdims=True) for score in scores]
    weights = [jnp.exp(score - peak) for score, peak in zip(scores, peaks)]
    totals = [jnp.sum(weight, axis=1, keepdims=True) for weight in weights]
    sums = []
    for weight, (_, place) in zip(weights, slots):
        high = weight.astype(jnp.bfloat16).astype(jnp.float32)
        low = weight - high
        parts = []
        for kv in range(kv_count):
            mine = slice(kv * group, (kv + 1) * group)
            both = jnp.dot(
                jnp.concatenate([high[mine], low[mine]], axis=0).astype(jnp.bfloat16),
                pages_ref[place, 1, :, kv * HEAD_DIM : (kv + 1) * HEAD_DIM],
                preferred_element_type=jnp.float32,
            )
            parts.append(both[:group] + both[group:])
        sums.append(jnp.concatenate(parts, axis=0))
    return list(zip(peaks, totals, sums))


def to_lanes(column, offset):
    shape = (column.shape[0], HEAD_DIM)
    at = lax.broadcasted_iota(jnp.int32, shape, 0) + offset
    lane = lax.broadcasted_iota(jnp.int32, shape, 1)
    return jnp.where(at == lane, column, 0.0)


def to_column(row, offset, heads):
    shape = (heads, HEAD_DIM)
    at = lax.broadcasted_iota(jnp.int32, shape, 0) + offset
    lane = lax.broadcasted_iota(jnp.int32, shape, 1)
    return jnp.sum(jnp.where(at == lane, row, 0.0), axis=1, keepdims=True)


def attend_kernel(heads, capacity, scale, payload_ref, pages_ref, out_ref):
    notes = payload_ref[capacity * heads :, :].astype(jnp.float32)
    slots = [
        (payload_ref[slot * heads : (slot + 1) * heads, :], notes[slot, 0].astype(jnp.int32))
        for slot in range(capacity)
    ]
    parts = page_parts(slots, pages_ref, scale)
    columns = [part[0] for part in parts] + [part[1] for part in parts]
    lane = lax.broadcasted_iota(jnp.int32, (heads, HEAD_DIM), 1)
    marks = columns[0]
    for at in range(1, 2 * capacity):
        marks = jnp.where(lane >= at * heads, columns[at], marks)
    head = lax.broadcasted_iota(jnp.int32, (heads, HEAD_DIM), 0)
    marks = jnp.where(lax.rem(lane, heads) == head, marks, 0.0)
    row = jnp.sum(marks, axis=0, keepdims=True)
    for slot, part in enumerate(parts):
        out_ref[slot * heads : (slot + 1) * heads, :] = part[2]
    out_ref[capacity * heads :, :] = jnp.broadcast_to(row, (TILE, HEAD_DIM))


def local_kernel(
    count, capacity, scale, owner_ref, length_ref, places_ref, queries_ref, fresh_ref, pages_ref,
    state_ref, bias_ref, rows
):
    seq_count = queries_ref.shape[0]
    heads = queries_ref.shape[1] // HEAD_DIM
    kv_count = fresh_ref.shape[2] // HEAD_DIM
    group = heads // kv_count
    spread_rows(queries_ref, rows)
    plan = slot_plan(owner_ref, length_ref, places_ref, count, capacity)
    local = page_parts(
        [(slot_rows(rows, seq, heads).astype(jnp.bfloat16), place) for seq, place, _ in plan[0]],
        pages_ref,
        scale,
    )
    line = lax.broadcasted_iota(jnp.int32, (TILE, HEAD_DIM), 0)
    lane = lax.broadcasted_iota(jnp.int32, (TILE, HEAD_DIM), 1)
    peaks = jnp.full((TILE, HEAD_DIM), NEVER, jnp.float32)
    totals = jnp.zeros((TILE, HEAD_DIM), jnp.float32)
    for seq in range(seq_count):
        query = rows[seq * heads : (seq + 1) * heads, :]

        def fresh(which):
            new = fresh_ref[seq, which : which + 1, :].astype(jnp.float32)
            return jnp.concatenate(
                [
                    jnp.broadcast_to(new[:, kv * HEAD_DIM : (kv + 1) * HEAD_DIM], (group, HEAD_DIM))
                    for kv in range(kv_count)
                ],
                axis=0,
            )

        own = jnp.sum(query * fresh(0), axis=1, keepdims=True) * scale
        highest = own
        for (at, _, used), (peak, _, _) in zip(plan[0], local):
            highest = jnp.maximum(highest, jnp.where((used > 0) & (at == seq), peak, NEVER))
        own_weight = jnp.exp(own - highest)
        denominator = own_weight
        numerator = own_weight * fresh(1)
        for (at, _, used), (peak, total, summed) in zip(plan[0], local):
            inside = (used > 0) & (at == seq)
            factor = jnp.exp(jnp.where(inside, peak - highest, NEVER))
            denominator = denominator + factor * total
            numerator = numerator + factor * summed
        state_ref[seq * heads : (seq + 1) * heads, :] = numerator
        high_row = jnp.sum(to_lanes(highest, 0), axis=0, keepdims=True)
        total_row = jnp.sum(to_lanes(denominator, 0), axis=0, keepdims=True)
        peaks = jnp.where((line == seq) & (lane < heads), high_row, peaks)
        totals = jnp.where(line == seq, total_row, totals)
    bias_ref[0:TILE, :] = peaks
    for step in range(1, REACH):
        bias = jnp.full((TILE, HEAD_DIM), NEVER, jnp.float32)
        for slot in range(capacity):
            at, _, used = plan[step][slot]
            mine = (line == at) & (lane // heads == slot) & (used > 0)
            bias = jnp.where(mine, 0.0, bias)
        bias_ref[step * TILE : (step + 1) * TILE, :] = bias
    bias_ref[REACH * TILE :, :] = totals


def combine_kernel(seq_count, capacity, state_ref, bias_ref, *refs):
    parts, out_ref, rows = refs[:-2], refs[-2], refs[-1]
    heads = out_ref.shape[1] // HEAD_DIM
    marks = [part[capacity * heads :, :] for part in parts]
    peaks = [bias_ref[0:TILE, :]] + [
        mark + bias_ref[(at + 1) * TILE : (at + 2) * TILE, :] for at, mark in enumerate(marks)
    ]
    totals = [bias_ref[REACH * TILE :, :]] + [
        pltpu.roll(mark, HEAD_DIM - capacity * heads, 1) for mark in marks
    ]

    def over_slots(tile, join):
        whole = tile
        for slot in range(1, capacity):
            whole = join(whole, pltpu.roll(tile, slot * heads, 1))
            whole = join(whole, pltpu.roll(tile, HEAD_DIM - slot * heads, 1))
        return whole

    highest = over_slots(functools.reduce(jnp.maximum, peaks), jnp.maximum)
    factors = [jnp.exp(peak - highest) for peak in peaks]
    share = functools.reduce(jnp.add, [factor * total for factor, total in zip(factors, totals)])
    inverse = 1.0 / over_slots(share, jnp.add)
    factors = [factor * inverse for factor in factors]
    for seq in range(seq_count):
        line = slice(seq, seq + 1)
        numerator = to_column(factors[0][line], 0, heads) * state_ref[seq * heads : (seq + 1) * heads, :]
        for factor, part in zip(factors[1:], parts):
            for slot in range(capacity):
                column = to_column(factor[line], slot * heads, heads)
                numerator = numerator + column * part[slot * heads : (slot + 1) * heads, :]
        rows[seq * heads : (seq + 1) * heads, :] = numerator
    for head in range(heads):
        out_ref[:, head * HEAD_DIM : (head + 1) * HEAD_DIM] = rows[
            pl.ds(head, seq_count, stride=heads), :
        ].astype(jnp.bfloat16)


def body(queries, new_kv, kv_pages, page_index, page_owner, seq_pages):
    count = lax.axis_size("store")
    seq_count, most_pages = page_index.shape
    capacity = seq_count * most_pages // REACH
    heads = queries.shape[1] // HEAD_DIM
    scale = HEAD_DIM ** (-0.5)
    rows = capacity * heads
    assert kv_pages.shape[0] <= FIELD and seq_count <= TILE
    assert 2 * rows <= HEAD_DIM and heads % TILE == 0
    sent = jax.ShapeDtypeStruct((rows + PACKED_TILE, HEAD_DIM), jnp.bfloat16)
    back = jax.ShapeDtypeStruct((rows + TILE, HEAD_DIM), jnp.float32)
    scratch = [pltpu.VMEM((seq_count * heads, HEAD_DIM), jnp.float32)]
    first = pl.pallas_call(
        first_kernel,
        out_shape=jax.ShapeDtypeStruct((TILE, HEAD_DIM), jnp.float32),
        out_specs=VMEM,
        compiler_params=PARAMS,
        cost_estimate=pl.CostEstimate(flops=2 * 10**9, bytes_accessed=0, transcendentals=0),
        name="first",
    )()
    payloads = pl.pallas_call(
        functools.partial(pack_kernel, count, capacity),
        out_shape=[sent] * (REACH - 1),
        in_specs=[VMEM] * 5,
        out_specs=[VMEM] * (REACH - 1),
        scratch_shapes=scratch,
        compiler_params=PARAMS,
        cost_estimate=pl.CostEstimate(flops=10**12, bytes_accessed=0, transcendentals=0),
        name="pack",
    )(first, page_owner, seq_pages, page_index, queries)
    attend = pl.pallas_call(
        functools.partial(attend_kernel, heads, capacity, scale),
        out_shape=back,
        in_specs=[VMEM] * 2,
        out_specs=VMEM,
        compiler_params=PARAMS,
        name="attend",
    )
    parts = []
    for step in range(1, REACH):
        payload = shifted(payloads[step - 1], "store", step)
        part = attend(payload, kv_pages)
        parts.append(shifted(part, "store", -step))
    state, bias = pl.pallas_call(
        functools.partial(local_kernel, count, capacity, scale),
        out_shape=[
            jax.ShapeDtypeStruct((seq_count * heads, HEAD_DIM), jnp.float32),
            jax.ShapeDtypeStruct(((REACH + 1) * TILE, HEAD_DIM), jnp.float32),
        ],
        in_specs=[SMEM] * 3 + [VMEM] * 3,
        out_specs=[VMEM] * 2,
        scratch_shapes=scratch,
        compiler_params=PARAMS,
        name="local",
    )(page_owner, seq_pages, page_index, queries, new_kv, kv_pages)
    return pl.pallas_call(
        functools.partial(combine_kernel, seq_count, capacity),
        out_shape=jax.ShapeDtypeStruct(queries.shape, queries.dtype),
        in_specs=[VMEM] * (1 + REACH),
        out_specs=VMEM,
        scratch_shapes=scratch,
        compiler_params=PARAMS,
        name="combine",
    )(state, bias, *parts)


def solution(mesh):
    in_specs = (
        P(("groups", "store"), "tensor"),
        P(("groups", "store"), None, "tensor"),
        P(("groups", "store"), None, None, "tensor"),
        P(("groups", "store"), None),
        P(("groups", "store"), None),
        P(("groups", "store")),
    )
    out_specs = P(("groups", "store"), "tensor")

    return jax.shard_map(body, mesh=mesh, in_specs=in_specs, out_specs=out_specs, check_vma=False)
```
